32 devices in a mesh: chan: 8 (over z, y), win: 4 (over x, core).
Axes of the slice: x: 2, y: 2, z: 4, core: 2. Of those that a mesh axis runs over, the one named last changes fastest.
Arguments:
- spectra: bfloat16 [4, 2048, 8192], P('win', 'chan'), may hold values from -6 to 6
- src_block: int32 [32], P('chan'), may hold values from 0 to 15, as said below
- rcv_block: int32 [32], P('chan'), may hold values from 0 to 15, as said below
- tile_count: int32 [8], P('chan'), may hold values from 1 to 4, as said below
Outputs:
- correlations: float32 [32, 128, 1024], P(('chan', 'win'))
The draws below stay inside these ranges and needn't reach their ends.
Inputs may be any that keep to these rules, and one draw needn't show every extreme that they name: src_block of a slot of index c of chan is a block of that index: c * 2 to c * 2 + 1. rcv_block lies from src_block to src_block + 4 and below 16; the offset 4 is reached by the first slot. `tile_count`: the first index of chan uses all 4 slots.
All inputs are finite; a program needn't handle non-finite values.
Results may differ from the reference program's by a relative error of at most 0.003.
Values may be sent and summed in bfloat16 or wider, within the bound.
No kernel may reach another device: no remote copies, remote signals or barrier semaphores. Data moves between devices by JAX's collectives and lax.ppermute only.
A program may use at most 128 MiB of HBM per device.

```python
import jax
import jax.numpy as jnp
from jax import lax

F = 4096
BLOCK = 128
CB_DEV = 2
R_BLK = 4
TMAX = 4
LAGS = 1024
NWIN = 4
NCH = 2048
SLOTS = 32
N_CHAN = 8


def tile_pairs(key):
    base = jax.random.fold_in(key, 7)
    first, second = jax.random.split(base)
    count = N_CHAN * TMAX
    owner = jnp.arange(count, dtype=jnp.int32) // TMAX
    local = jax.random.randint(first, (count,), 0, CB_DEV, dtype=jnp.int32)
    offset = jax.random.randint(second, (count,), 0, R_BLK + 1, dtype=jnp.int32)
    offset = offset.at[0].set(R_BLK)
    source = owner * CB_DEV + local
    receiver = jnp.minimum(source + offset, CB_DEV * N_CHAN - 1)
    return (source, receiver)


def draw_src_block(key, part):
    return tile_pairs(key)[0]


def draw_rcv_block(key, part):
    return tile_pairs(key)[1]


def draw_tile_count(key, part):
    counts = jax.random.randint(jax.random.fold_in(key, 11), (N_CHAN,), 1, TMAX + 1, dtype=jnp.int32)
    return counts.at[0].set(TMAX)


def block_levels(key, dims, shards, least, top_value):
    def one(axis_at, parts):
        heights = jax.random.uniform(jax.random.fold_in(jax.random.fold_in(key, 6), axis_at), (parts,), jnp.float32, least / len(shards), top_value / len(shards))
        return jnp.repeat(jnp.exp(heights), dims[axis_at] // parts).reshape((-1,) + (1,) * (len(dims) - axis_at - 1))

    gain = one(*shards[0])
    for cut in shards[1:]:
        gain = gain * one(*cut)
    return gain


def noise(key, shape, spread, reach, cuts=(), held_as=jnp.bfloat16):
    level = block_levels(key, shape, cuts, -0.22, 0.18) if cuts else 1.0
    array = jax.random.normal(key, shape, jnp.float32) * spread * level
    return jnp.minimum(jnp.maximum(array, -reach), reach).astype(held_as)


def setup_inputs(seed: int = 0) -> dict:
    keys = jax.random.split(jax.random.key(seed), 5)
    return {
        "spectra": noise(keys[0], (NWIN, NCH, 2 * F), 1.0, 6.0, ((0, 4), (1, 8))),
        "src_block": draw_src_block(jax.random.fold_in(keys[4], 71), 0),
        "rcv_block": draw_rcv_block(jax.random.fold_in(keys[4], 71), 0),
        "tile_count": draw_tile_count(jax.random.fold_in(keys[4], 71), 0),
    }


def whiten(block):
    half = block.shape[-1] // 2
    real_part = block[..., :half].astype(jnp.float32)
    imag_part = block[..., half:].astype(jnp.float32)
    power = real_part * real_part + imag_part * imag_part
    level = lax.optimization_barrier(jnp.mean(power, axis=-1, keepdims=True))
    factor = 1.0 / jnp.sqrt(power + level + 1e-06)
    return jnp.concatenate([real_part * factor, imag_part * factor], axis=-1).astype(jnp.bfloat16)

def cross_spectrum(source, receiver):
    half = source.shape[-1] // 2
    s_re = source[..., :half].astype(jnp.float32)
    s_im = source[..., half:].astype(jnp.float32)
    r_re = receiver[..., :half].astype(jnp.float32)
    r_im = receiver[..., half:].astype(jnp.float32)
    return jnp.concatenate([s_re * r_re + s_im * r_im, s_re * r_im - s_im * r_re], axis=-1).astype(jnp.bfloat16)

def lag_table(freqs, lags):
    nfft = 2 * freqs
    fidx = jnp.arange(freqs, dtype=jnp.int32)[:, None]
    shift = jnp.arange(lags, dtype=jnp.int32)[None, :] - lags // 2
    phase = jnp.mod(fidx * shift, nfft).astype(jnp.float32) * (2.0 * jnp.pi / nfft)
    scale = 1.0 / jnp.sqrt(jnp.float32(freqs))
    return jnp.concatenate([jnp.cos(phase) * scale, -jnp.sin(phase) * scale], axis=0).astype(jnp.bfloat16)

def reference(spectra, src_block, rcv_block, tile_count):
    white = lax.map(whiten, spectra)
    table = lag_table(F, LAGS).astype(jnp.float32)

    def one_slot(slot):
        owner = slot // TMAX
        place = slot % TMAX
        source = lax.dynamic_slice_in_dim(white, (src_block[slot] * BLOCK).astype(jnp.int32), BLOCK, 1)
        receiver = lax.dynamic_slice_in_dim(white, (rcv_block[slot] * BLOCK).astype(jnp.int32), BLOCK, 1)
        cross = cross_spectrum(source, receiver).astype(jnp.float32)
        used = place < tile_count[owner]
        cross = jnp.where(used, cross, jnp.zeros_like(cross))
        return jnp.einsum('wbf,fl->bl', cross, table)
    return lax.map(one_slot, jnp.arange(SLOTS, dtype=jnp.int32))
```

```python
import functools

import jax
import jax.numpy as jnp
from jax import lax
from jax.experimental import pallas as pl
from jax.experimental.pallas import tpu as pltpu
from jax.sharding import PartitionSpec as P

CB_DEV = 2
LAGS = 1024
CHUNKS = 2
MIB = 1 << 20

VMEM = pl.BlockSpec(memory_space=pltpu.VMEM)
SMEM = pl.BlockSpec(memory_space=pltpu.SMEM)
ANY = pl.BlockSpec(memory_space=pl.ANY)

OWN_L, OWN_U, SIDE, ABOVE, BELOW = range(5)


def whiten_kernel(meta_ref, x_ref, low_ref, up_ref, side_ref):
    freqs = x_ref.shape[-1] // 2
    half = freqs // 2
    re = x_ref[:, :freqs].astype(jnp.float32)
    im = x_ref[:, freqs:].astype(jnp.float32)
    power = re * re + im * im
    level = jnp.sum(power, axis=-1, keepdims=True) * (1.0 / freqs)
    factor = lax.rsqrt(power + level + 1e-06)
    re = (re * factor).astype(jnp.bfloat16)
    im = (im * factor).astype(jnp.bfloat16)
    low_ref[:, :half] = re[:, :half]
    low_ref[:, half:] = im[:, :half]
    up_ref[:, :half] = re[:, half:]
    up_ref[:, half:] = im[:, half:]
    odd = meta_ref[meta_ref.shape[0] - 2] % 2

    @pl.when(odd == 0)
    def _():
        side_ref[...] = up_ref[...]

    @pl.when(odd == 1)
    def _():
        side_ref[...] = low_ref[...]


def whiten_chunk(meta, blocks, start, rows):
    count, _, width = blocks.shape
    tile = 16
    first = start // tile
    out = jax.ShapeDtypeStruct((count, rows, width // 2), jnp.bfloat16)
    spec = pl.BlockSpec((None, tile, width // 2), lambda b, i: (b, i, 0))
    return pl.pallas_call(
        whiten_kernel,
        name="whiten",
        grid=(count, rows // tile),
        in_specs=[SMEM, pl.BlockSpec((None, tile, width), lambda b, i: (b, i + first, 0))],
        out_specs=[spec] * 3,
        out_shape=[out] * 3,
        compiler_params=pltpu.CompilerParams(vmem_limit_bytes=16 * MIB),
        cost_estimate=pl.CostEstimate(
            flops=20 * count * rows * width, bytes_accessed=5 * count * rows * width, transcendentals=0
        ),
    )(meta, blocks)


def table_kernel(step, freqs, table_ref, cin_ref, sin_ref, cout_ref, sout_ref):
    half = freqs // 2
    lags = table_ref.shape[-1]
    nfft = 2 * freqs
    scale = float(freqs) ** -0.5

    def base(count, stride):
        shape = (count, lags)
        f = lax.broadcasted_iota(jnp.int32, shape, 0) * stride
        shift = lax.broadcasted_iota(jnp.int32, shape, 1) - lags // 2
        phase = ((f * shift) & (nfft - 1)).astype(jnp.float32) * (2.0 * jnp.pi / nfft)
        return jnp.cos(phase), jnp.sin(phase)

    fine_cos, fine_sin = base(step, 1)
    cin_ref[...] = fine_cos * scale
    sin_ref[...] = fine_sin * scale
    coarse_cos, coarse_sin = base(freqs // step, step)
    cout_ref[...] = coarse_cos
    sout_ref[...] = coarse_sin
    per_half = half // step
    tile, cols = 16, 512

    def fill(at, carry):
        which = at // per_half
        row = (at % per_half) * step
        for col in range(0, lags, cols):
            where = slice(col, col + cols)
            cos_at = cout_ref[pl.ds(at, 1), where]
            sin_at = sout_ref[pl.ds(at, 1), where]
            for inner in range(0, step, tile):
                cos_in = cin_ref[inner : inner + tile, where]
                sin_in = sin_ref[inner : inner + tile, where]
                to = pl.multiple_of(row + inner, tile)
                table_ref[which, pl.ds(to, tile), where] = (
                    cos_at * cos_in - sin_at * sin_in
                ).astype(jnp.bfloat16)
                table_ref[which, pl.ds(half + to, tile), where] = (
                    -(sin_at * cos_in + cos_at * sin_in)
                ).astype(jnp.bfloat16)
        return carry

    lax.fori_loop(0, freqs // step, fill, 0)


def lag_table(freqs, lags):
    step = 64
    return pl.pallas_call(
        functools.partial(table_kernel, step, freqs),
        name="lag_table",
        out_specs=VMEM,
        out_shape=jax.ShapeDtypeStruct((2, freqs, lags), jnp.bfloat16),
        scratch_shapes=[pltpu.VMEM((step, lags), jnp.float32)] * 2
        + [pltpu.VMEM((freqs // step, lags), jnp.float32)] * 2,
        compiler_params=pltpu.CompilerParams(vmem_limit_bytes=24 * MIB),
        cost_estimate=pl.CostEstimate(flops=14 * freqs * lags, bytes_accessed=4 * freqs * lags, transcendentals=0),
    )()


def pairs_kernel(
    slots, own_ref, side_meta_ref, below_meta_ref,
    low, up, side, above, below, table_ref,
    keep_ref, send_ref,
    bufs, cross, product, total, slot_of, sems,
):
    copies = [
        pltpu.make_async_copy(src, bufs.at[i], sems.at[i])
        for i, src in enumerate((low, up, side, above, below))
    ]
    for copy in copies:
        copy.start()
    rows = bufs.shape[2]
    half = bufs.shape[3] // 2
    lags = table_ref.shape[-1]
    chan = own_ref[2 * slots + 1]
    win = own_ref[2 * slots + 2]
    odd = chan % 2
    total[...] = jnp.zeros_like(total)
    for copy in copies:
        copy.wait()

    def job_of(which, at):
        group, place = at // slots, at % slots
        pick = lambda i: jnp.where(
            group == 0, own_ref[i], jnp.where(group == 1, side_meta_ref[i], below_meta_ref[i])
        )
        owner = jnp.where(group == 0, chan, jnp.where(group == 1, chan + 1 - 2 * odd, chan - 2))
        src, rcv = pick(place), pick(slots + place)
        used = place < pick(2 * slots)
        gap = rcv // CB_DEV - owner
        if which == 0:
            here = jnp.where(
                group == 0,
                jnp.where(gap == 1, odd == 0, gap >= 0),
                jnp.logical_and(jnp.logical_and(group == 1, odd == 0), gap == 1),
            )
            source = jnp.where(group == 0, OWN_L, SIDE)
            receiver = jnp.where(
                group == 0, jnp.where(gap == 0, OWN_L, jnp.where(gap == 1, SIDE, ABOVE)), ABOVE
            )
        else:
            here = jnp.where(
                group == 0,
                gap == 0,
                jnp.where(
                    group == 1,
                    jnp.logical_and(odd == 1, gap == 1),
                    jnp.where(gap == 1, odd == 1, gap == 2),
                ),
            )
            source = jnp.where(group == 0, OWN_U, jnp.where(group == 1, SIDE, BELOW))
            receiver = jnp.where(jnp.logical_and(group == 2, gap == 1), SIDE, OWN_U)
        return jnp.logical_and(used, here), source, src % CB_DEV, receiver, rcv % CB_DEV

    cols = 256
    tile = 16
    group_rows = slots * rows

    for which in range(2):
        groups = 2 if which == 0 else 3

        def build(at, count):
            valid, source, s_blk, receiver, r_blk = job_of(which, at)

            @pl.when(valid)
            def _():
                slot_of[count] = at
                for col in range(0, half, cols):
                    def one(i, carry):
                        r = pl.multiple_of(i * tile, tile)
                        to = pl.multiple_of(count * rows + i * tile, tile)
                        s_re = bufs[source, s_blk, pl.ds(r, tile), col : col + cols].astype(jnp.float32)
                        s_im = bufs[source, s_blk, pl.ds(r, tile), half + col : half + col + cols].astype(jnp.float32)
                        r_re = bufs[receiver, r_blk, pl.ds(r, tile), col : col + cols].astype(jnp.float32)
                        r_im = bufs[receiver, r_blk, pl.ds(r, tile), half + col : half + col + cols].astype(jnp.float32)
                        cross[pl.ds(to, tile), col : col + cols] = (s_re * r_re + s_im * r_im).astype(jnp.bfloat16)
                        cross[pl.ds(to, tile), half + col : half + col + cols] = (s_re * r_im - s_im * r_re).astype(jnp.bfloat16)
                        return carry
                    lax.fori_loop(0, rows // tile, one, 0)

            return count + valid.astype(jnp.int32)

        jobs = lax.fori_loop(0, groups * slots, build, 0)

        def multiply(m, carry):
            base = pl.multiple_of(m * group_rows, tile)

            def column(n, inner):
                at = pl.multiple_of(n * cols, cols)
                product[:, pl.ds(at, cols)] = jnp.dot(
                    cross[pl.ds(base, group_rows), :],
                    table_ref[which, :, pl.ds(at, cols)],
                    preferred_element_type=jnp.float32,
                )
                return inner

            lax.fori_loop(0, lags // cols, column, 0)
            for j in range(slots):
                @pl.when(m * slots + j < jobs)
                def _():
                    slot = slot_of[m * slots + j]
                    total[slot] += product[j * rows : (j + 1) * rows, :]
            return carry

        lax.fori_loop(0, (jobs + slots - 1) // slots, multiply, 0)

    low_bit, high_bit = win % 2, win // 2
    for group in range(3):
        for far in range(2):
            high = jnp.where(far == 0, high_bit, 1 - high_bit)
            mine = group * slots + 2 * high + low_bit
            other = group * slots + 2 * high + 1 - low_bit
            keep_ref[group, far] = total[mine]
            send_ref[group, far] = total[other].astype(jnp.bfloat16)


def pairs_chunk(slots, metas, parts, table):
    blocks, rows, width = parts[0].shape
    lags = table.shape[-1]
    shape = (3, slots // 2, rows, lags)
    return pl.pallas_call(
        functools.partial(pairs_kernel, slots),
        name="pairs",
        in_specs=[SMEM] * 3 + [ANY] * 5 + [VMEM],
        out_specs=[VMEM] * 2,
        out_shape=[jax.ShapeDtypeStruct(shape, jnp.float32), jax.ShapeDtypeStruct(shape, jnp.bfloat16)],
        scratch_shapes=[
            pltpu.VMEM((5, blocks, rows, width), jnp.bfloat16),
            pltpu.VMEM((3 * slots * rows, width), jnp.bfloat16),
            pltpu.VMEM((slots * rows, lags), jnp.float32),
            pltpu.VMEM((3 * slots, rows, lags), jnp.float32),
            pltpu.SMEM((3 * slots,), jnp.int32),
            pltpu.SemaphoreType.DMA((5,)),
        ],
        compiler_params=pltpu.CompilerParams(vmem_limit_bytes=44 * MIB),
        cost_estimate=pl.CostEstimate(
            flops=2 * 6 * rows * width * lags, bytes_accessed=10 * blocks * rows * width, transcendentals=0
        ),
    )(*metas, *parts, table)


def split_kernel(keep_ref, got_ref, own_ref, *out_refs):
    for group in range(3):
        for far in range(2):
            value = keep_ref[group, far] + got_ref[group, far].astype(jnp.float32)
            if group == 0 and far == 0:
                own_ref[...] = value
            else:
                out_refs[2 * group + far - 1][...] = value.astype(jnp.bfloat16)


def split_chunk(keep, got):
    rows, lags = keep.shape[2:]
    return pl.pallas_call(
        split_kernel,
        name="split",
        in_specs=[VMEM] * 2,
        out_specs=[VMEM] * 6,
        out_shape=[jax.ShapeDtypeStruct((rows, lags), jnp.float32)]
        + [jax.ShapeDtypeStruct((rows, lags), jnp.bfloat16)] * 5,
        compiler_params=pltpu.CompilerParams(vmem_limit_bytes=24 * MIB),
        cost_estimate=pl.CostEstimate(flops=12 * rows * lags, bytes_accessed=50 * rows * lags, transcendentals=0),
    )(keep, got)


def final_kernel(per, *refs):
    out_ref = refs[-1]
    at = 0
    for i in range(0, len(refs) - 1, per):
        value = refs[i][...]
        for ref in refs[i + 1 : i + per]:
            value = value + ref[...].astype(jnp.float32)
        out_ref[0, at : at + value.shape[0], :] = value
        at += value.shape[0]


def final_sum(chunks, rows, lags):
    flat = [x for chunk in chunks for x in chunk]
    return pl.pallas_call(
        functools.partial(final_kernel, len(chunks[0])),
        name="final_sum",
        in_specs=[VMEM] * len(flat),
        out_specs=VMEM,
        out_shape=jax.ShapeDtypeStruct((1, rows, lags), jnp.float32),
        compiler_params=pltpu.CompilerParams(vmem_limit_bytes=24 * MIB),
    )(*flat)


def body(chans, wins, spectra, src_block, rcv_block, tile_count):
    slots = src_block.shape[0]
    chan, win = lax.axis_index("chan"), lax.axis_index("win")
    meta = jnp.concatenate(
        [src_block, rcv_block, tile_count, jnp.stack([chan, win]).astype(jnp.int32)]
    )
    down = [(c, c - 2) for c in range(2, chans)]
    upward = [(c, c + 2) for c in range(chans - 2)]
    swap = [(c, c ^ 1) for c in range(chans)]
    metas = [meta, lax.ppermute(meta, "chan", swap), lax.ppermute(meta, "chan", upward)]

    def to_owner(value, chan_pairs, far):
        pairs = [
            (a * wins + w, b * wins + (w ^ (2 * far))) for a, b in chan_pairs for w in range(wins)
        ]
        return lax.ppermute(value, ("chan", "win"), pairs)

    stay = [(c, c) for c in range(chans)]
    block_rows = spectra.shape[1] // CB_DEV
    blocks = spectra.reshape(CB_DEV, block_rows, spectra.shape[2])
    rows = block_rows // CHUNKS
    chunks = []
    for start in range(0, block_rows, rows):
        low, up, side = whiten_chunk(meta, blocks, start, rows)
        chunks.append(
            (
                low,
                up,
                lax.ppermute(side, "chan", swap),
                lax.ppermute(low, "chan", down),
                lax.ppermute(up, "chan", upward),
            )
        )
    table = lag_table(spectra.shape[2] // 2, LAGS)
    done = []
    for parts in chunks:
        keep, send = pairs_chunk(slots, metas, parts, table)
        got = lax.ppermute(send, "win", [(w, w ^ 1) for w in range(wins)])
        own, own_far, side_near, side_far, below_near, below_far = split_chunk(keep, got)
        done.append(
            (
                own,
                to_owner(own_far, stay, 1),
                to_owner(side_near, swap, 0),
                to_owner(side_far, swap, 1),
                to_owner(below_near, down, 0),
                to_owner(below_far, down, 1),
            )
        )
    return final_sum(done, block_rows, LAGS)


def solution(mesh):
    in_specs = (P("win", "chan", None), P("chan"), P("chan"), P("chan"))
    out_specs = P(("chan", "win"), None, None)
    return jax.shard_map(
        functools.partial(body, mesh.shape["chan"], mesh.shape["win"]),
        mesh=mesh, in_specs=in_specs, out_specs=out_specs, check_vma=False,
    )
```
